256 devices in a mesh: lat: 16 (over z_lo, y, core), mem: 16 (over x, z_hi).
Axes of the slice: x: 4, y: 4, z: 8 (z_hi: 4, z_lo: 2; z = z_hi * 2 + z_lo), core: 2. Of those that a mesh axis runs over, the one named last changes fastest.
Arguments:
- predicted_fields: bfloat16 [16, 8, 768, 1440], P('mem', None, 'lat'), may hold values from -6 to 6
- weighted_polynomial: bfloat16 [768, 768, 768], P(('lat', 'mem')), may hold values from -0.21875 to 0.21875
- truth_spectrum: float32 [768, 2, 8, 768], P(('lat', 'mem')), may hold values from -5 to 5
- field_importance: float32 [8], replicated, may hold values from 0.3 to 3
- parallels_in_zone: int32 [16], replicated, may hold values from 1 to 48, as said below
- order_of_place: int32 [768], replicated, may hold values from 0 to 767, each once
Outputs:
- field_grad: bfloat16 [16, 8, 768, 1440], P('mem', None, 'lat')
The draws below stay inside these ranges and needn't reach their ends.
Inputs may be any that keep to these rules, and one draw needn't show every extreme that they name: Band b holds latitude rows b * 48 to b * 48 + parallels_in_zone[b] - 1 of the padded grid; the others are padding; the entries sum to 721. Slot s holds order order_of_place[s] if it is at most 720; a slot with a larger entry is empty.
All inputs are finite; a program needn't handle non-finite values.
Results may differ from the reference program's by a relative error of at most 0.0084.
Values may be sent and summed in bfloat16 or wider, within the bound.
No kernel may reach another device: no remote copies, remote signals or barrier semaphores. Data moves between devices by JAX's collectives and lax.ppermute only.
A program may use at most 64 MiB of HBM per device.

```python
import math
import jax
import jax.numpy as jnp
from jax import lax

MERIDIAN_TOTAL = 1440
NLAT = 721
LMAX = 720
FIELD_KINDS = 8
MEMBER_TOTAL = 16
LAT_DEV = 48
PARALLEL_LINES = 768
ORDER_PLACES = 768
HARMONIC_DEGREES = 768
N_LAT = 16


def draw_parallels_in_zone(key, part):
    others_count = max(N_LAT - 1, 1)
    remaining = NLAT - LAT_DEV
    base_rows = remaining // others_count
    leftover = remaining % others_count
    spread = max(min(base_rows - 1, LAT_DEV - 1 - base_rows), 0) // 2
    key_extra = jax.random.fold_in(key, 11)
    key_shift = jax.random.fold_in(key, 23)
    key_order = jax.random.fold_in(key, 37)
    ranking = jax.random.permutation(key_extra, jnp.arange(others_count, dtype=jnp.int32))
    extras = (ranking < leftover).astype(jnp.int32)
    shifts = jax.random.randint(key_shift, (others_count,), -spread, spread + 1, dtype=jnp.int32)
    balanced = shifts - jnp.roll(shifts, 1)
    others = base_rows + extras + balanced
    full_band = jnp.full((1,), LAT_DEV, dtype=jnp.int32)
    whole = jnp.concatenate([full_band, others[:N_LAT - 1]]).astype(jnp.int32)
    return jax.random.permutation(key_order, whole).astype(jnp.int32)


def levels(own_key, dims, cuts, low, top_value):
    loudness = 1.0
    for axis_at, shards_of in cuts:
        steps = jax.random.uniform(jax.random.fold_in(jax.random.fold_in(own_key, 6), axis_at), (shards_of,), jnp.float32, low / len(cuts), top_value / len(cuts))
        loudness = loudness * jnp.repeat(jnp.exp(steps), dims[axis_at] // shards_of).reshape((-1,) + (1,) * (len(dims) - 1 - axis_at))
    return loudness


def scatter_about(stream_key, extent, deviation, most, pieces=(), kind=jnp.bfloat16):
    level = levels(stream_key, extent, pieces, -0.22, 0.18) if pieces else 1.0
    entries = jax.random.normal(stream_key, extent, jnp.float32) * deviation * level
    return jnp.minimum(jnp.maximum(entries, -most), most).astype(kind)


def setup_inputs(seed: int = 0) -> dict:
    keys = jax.random.split(jax.random.key(seed), 7)
    predicted_fields = scatter_about(keys[0], (MEMBER_TOTAL, FIELD_KINDS, PARALLEL_LINES, MERIDIAN_TOTAL), 1.0, 6.0, ((0, 16), (2, 16)))
    weighted_polynomial = scatter_about(keys[1], (ORDER_PLACES, PARALLEL_LINES, HARMONIC_DEGREES), NLAT ** -0.5, 0.21875, ((0, 256),))
    truth_spectrum = scatter_about(keys[2], (ORDER_PLACES, 2, FIELD_KINDS, HARMONIC_DEGREES), 0.7, 5.0, ((0, 256),), jnp.float32)
    field_importance = jnp.clip(jnp.exp(jax.random.uniform(keys[3], (FIELD_KINDS,), jnp.float32, math.log(0.3), math.log(3.0))), 0.3, 3.0)
    parallels_in_zone = draw_parallels_in_zone(jax.random.fold_in(keys[6], 71), 0)
    order_of_place = jax.random.permutation(keys[5], ORDER_PLACES).astype(jnp.int32)
    return {"predicted_fields": predicted_fields, "weighted_polynomial": weighted_polynomial, "truth_spectrum": truth_spectrum, "field_importance": field_importance, "parallels_in_zone": parallels_in_zone, "order_of_place": order_of_place}


EPS = 0.01

def dft_table(orders, meridian_number):
    longitude = jnp.arange(meridian_number, dtype=jnp.int32)
    product = longitude[:, None] * orders[None, :].astype(jnp.int32) % meridian_number
    angle = 2.0 * math.pi / meridian_number * product.astype(jnp.float32)
    inuse_markers = (orders <= LMAX).astype(jnp.float32) / math.sqrt(meridian_number)
    table = jnp.stack([jnp.cos(angle) * inuse_markers[None, :], -jnp.sin(angle) * inuse_markers[None, :]], axis=2)
    return table.reshape(meridian_number, 2 * orders.shape[0]).astype(jnp.bfloat16)

def kernel_grad(apart):
    return apart / jnp.sqrt(apart[0:1] * apart[0:1] + apart[1:2] * apart[1:2] + EPS)

def reference(predicted_fields, weighted_polynomial, truth_spectrum, field_importance, parallels_in_zone, order_of_place):
    place = jnp.arange(PARALLEL_LINES, dtype=jnp.int32)
    lengths = parallels_in_zone[place // LAT_DEV]
    inuse_markers = (place % LAT_DEV < lengths).astype(jnp.bfloat16)
    zeroed_entries = predicted_fields * inuse_markers[None, None, :, None]
    table = dft_table(order_of_place, MERIDIAN_TOTAL)
    harmonic_modes = jnp.einsum('mcpn,nk->kmcp', zeroed_entries.astype(jnp.float32), table.astype(jnp.float32))
    harmonic_modes = harmonic_modes.astype(jnp.bfloat16).reshape(ORDER_PLACES, 2, MEMBER_TOTAL, FIELD_KINDS, PARALLEL_LINES)
    degree = jnp.arange(HARMONIC_DEGREES, dtype=jnp.int32)

    def per_slot(items):
        spec, table_slot, observed, order = items
        valid = ((degree >= order) & (degree <= LMAX)).astype(jnp.float32)
        coeffs = jnp.einsum('rmcp,pl->rmcl', spec.astype(jnp.float32), table_slot.astype(jnp.float32))
        coeffs = coeffs * valid[None, None, None, :]
        term = kernel_grad(coeffs - observed[:, None])
        apart = coeffs[:, :, None] - coeffs[:, None, :]
        pair = lax.optimization_barrier(jnp.sum(apart / jnp.sqrt(apart[0:1] * apart[0:1] + apart[1:2] * apart[1:2] + EPS), axis=2))
        grads = field_importance[None, None, :, None] * valid[None, None, None, :] * (term - pair / MEMBER_TOTAL)
        grads = grads.astype(jnp.bfloat16)
        back = jnp.einsum('rmcl,pl->rmcp', grads.astype(jnp.float32), table_slot.astype(jnp.float32))
        return back.astype(jnp.bfloat16)
    inverse_results = lax.map(per_slot, (harmonic_modes, weighted_polynomial, truth_spectrum, order_of_place))
    inverse_results = inverse_results.reshape(2 * ORDER_PLACES, MEMBER_TOTAL, FIELD_KINDS, PARALLEL_LINES)
    field = jnp.einsum('kmcp,nk->mcpn', inverse_results.astype(jnp.float32), table.astype(jnp.float32))
    field = field * inuse_markers.astype(jnp.float32)[None, None, :, None]
    return field.astype(jnp.bfloat16)
```

```python
import functools
import math

import jax
import jax.numpy as jnp
from jax import lax
from jax.experimental import pallas as pl
from jax.experimental.pallas import tpu as pltpu
from jax.sharding import PartitionSpec as P

LMAX = 720
EPS = 0.01
LANES = 128


def angle_tables(orders, steps, meridian_number):
    product = orders[..., None] * steps % meridian_number
    angle = 2.0 * math.pi / meridian_number * product.astype(jnp.float32)
    return jnp.cos(angle), jnp.sin(angle)


def fill_tables(coarse_ref, fine_ref, cos_ref, sin_ref):
    fine_cos, fine_sin = fine_ref[0, 0], fine_ref[0, 1]
    meridian_number = cos_ref.shape[1]
    for j in range(pl.cdiv(meridian_number, LANES)):
        wide = min(LANES, meridian_number - j * LANES)
        coarse_cos = coarse_ref[0, 0, :, j : j + 1]
        coarse_sin = coarse_ref[0, 1, :, j : j + 1]
        cosine = coarse_cos * fine_cos - coarse_sin * fine_sin
        sine = -(coarse_sin * fine_cos + coarse_cos * fine_sin)
        at = slice(j * LANES, j * LANES + wide)
        cos_ref[:, at] = cosine[:, :wide].astype(jnp.bfloat16)
        sin_ref[:, at] = sine[:, :wide].astype(jnp.bfloat16)


def forward_kernel(rows_ref, live_ref, coarse_ref, fine_ref, out_ref, cos_ref, sin_ref):
    fill_tables(coarse_ref, fine_ref, cos_ref, sin_ref)
    rows = rows_ref[...]
    width = rows.shape[0]
    for part, table in enumerate((cos_ref, sin_ref)):
        modes = lax.dot_general(
            table[...], rows, (((1,), (1,)), ((), ())), preferred_element_type=jnp.float32
        )
        out_ref[:, part * width : (part + 1) * width] = (modes * live_ref[...]).astype(jnp.bfloat16)


def inverse_kernel(own_ref, back_ref, coarse_ref, fine_ref, out_ref, cos_ref, sin_ref, total_ref):
    slot = pl.program_id(0)
    fill_tables(coarse_ref, fine_ref, cos_ref, sin_ref)
    kinds, height, meridian_number = out_ref.shape
    width = kinds * height
    term = jnp.zeros((width, meridian_number), jnp.float32)
    for part, table in enumerate((cos_ref, sin_ref)):
        term = term + lax.dot_general(
            back_ref[:, part * width : (part + 1) * width],
            table[...],
            (((0,), (0,)), ((), ())),
            preferred_element_type=jnp.float32,
        )

    @pl.when(slot == 0)
    def _():
        total_ref[...] = term

    @pl.when(slot > 0)
    def _():
        total_ref[...] += term

    @pl.when(slot == pl.num_programs(0) - 1)
    def _():
        place = lax.broadcasted_iota(jnp.int32, (height, meridian_number), 0)
        live = (place < own_ref[0]).astype(jnp.float32)
        for kind in range(kinds):
            rows = total_ref[kind * height : (kind + 1) * height, :]
            out_ref[kind] = (rows * live).astype(jnp.bfloat16)


def kernel_grad(first, second):
    scale = lax.rsqrt(first * first + second * second + EPS)
    return first * scale, second * scale


def score_kernel(
    bands, members, kinds, height,
    spec_ref, poly_ref, truth_ref, weight_ref, out_ref, modes_ref, coeff_ref,
):
    width = kinds * height
    half = kinds * members
    tiles = coeff_ref.shape[0]

    for band in range(bands):
        source = slice(band * members, (band + 1) * members)
        for part in range(2):
            for kind in range(kinds):
                row = (part * kinds + kind) * members
                at = part * width + kind * height
                modes_ref[row : row + members, band * height : (band + 1) * height] = spec_ref[
                    source, at : at + height
                ]

    poly = poly_ref[0]
    coeffs = jnp.dot(modes_ref[...], poly, preferred_element_type=jnp.float32)
    for tile in range(tiles):
        coeff_ref[tile] = coeffs[:, tile * LANES : (tile + 1) * LANES]

    def per_tile(tile, carry):
        real = [coeff_ref[tile, pl.ds(m, kinds, stride=members), :] for m in range(members)]
        imag = [coeff_ref[tile, pl.ds(half + m, kinds, stride=members), :] for m in range(members)]
        pair_real = [jnp.zeros_like(real[0]) for _ in range(members)]
        pair_imag = [jnp.zeros_like(real[0]) for _ in range(members)]
        lanes = pl.ds(pl.multiple_of(tile * LANES, LANES), LANES)
        truth_real, truth_imag = truth_ref[0, 0, :, lanes], truth_ref[0, 1, :, lanes]
        weight = weight_ref[0, :, lanes]
        for m in range(members):
            for j in range(m + 1, members):
                first, second = kernel_grad(real[m] - real[j], imag[m] - imag[j])
                pair_real[m] = pair_real[m] + first
                pair_imag[m] = pair_imag[m] + second
                pair_real[j] = pair_real[j] - first
                pair_imag[j] = pair_imag[j] - second
            first, second = kernel_grad(real[m] - truth_real, imag[m] - truth_imag)
            coeff_ref[tile, pl.ds(m, kinds, stride=members), :] = weight * (
                first - pair_real[m] * (1.0 / members)
            )
            coeff_ref[tile, pl.ds(half + m, kinds, stride=members), :] = weight * (
                second - pair_imag[m] * (1.0 / members)
            )
        return carry

    lax.fori_loop(0, tiles, per_tile, 0)

    back = jnp.zeros(modes_ref.shape, jnp.float32)
    for tile in range(tiles):
        back = back + lax.dot_general(
            coeff_ref[tile].astype(jnp.bfloat16),
            poly[:, tile * LANES : (tile + 1) * LANES],
            (((1,), (1,)), ((), ())),
            preferred_element_type=jnp.float32,
        )
    modes_ref[...] = back.astype(jnp.bfloat16)

    for band in range(bands):
        target = slice(band * members, (band + 1) * members)
        for part in range(2):
            for kind in range(kinds):
                row = (part * kinds + kind) * members
                at = part * width + kind * height
                out_ref[target, at : at + height] = modes_ref[
                    row : row + members, band * height : (band + 1) * height
                ]


def local(
    predicted_fields,
    weighted_polynomial,
    truth_spectrum,
    field_importance,
    parallels_in_zone,
    order_of_place,
):
    _, kinds, height, meridian_number = predicted_fields.shape
    slot_dev, places, degrees = weighted_polynomial.shape
    slots = order_of_place.shape[0]
    devices = slots // slot_dev
    bands, members = lax.axis_size("lat"), lax.axis_size("mem")
    width = kinds * height
    own_rows = parallels_in_zone[lax.axis_index("lat")]
    live = (jnp.arange(width, dtype=jnp.int32) % height < own_rows).astype(jnp.float32)[None, :]

    orders = order_of_place.reshape(devices, slot_dev).T
    used = (orders <= LMAX).astype(jnp.float32)[:, None, :, None] / math.sqrt(meridian_number)
    fine = jnp.stack(angle_tables(orders, jnp.arange(LANES), meridian_number), axis=1) * used
    coarse = jnp.stack(
        angle_tables(orders, LANES * jnp.arange(LANES), meridian_number), axis=1
    )
    table_specs = [
        pl.BlockSpec((1, 2, devices, LANES), lambda s: (s, 0, 0, 0)),
        pl.BlockSpec((1, 2, devices, LANES), lambda s: (s, 0, 0, 0)),
    ]
    table_scratch = [
        pltpu.VMEM((devices, meridian_number), jnp.bfloat16),
        pltpu.VMEM((devices, meridian_number), jnp.bfloat16),
    ]
    exchange_shape = jax.ShapeDtypeStruct((devices, slot_dev * 2 * width), jnp.bfloat16)
    slab = pl.BlockSpec((devices, 2 * width), lambda s: (0, s))

    rows = predicted_fields.reshape(width, meridian_number)
    modes = pl.pallas_call(
        forward_kernel,
        grid=(slot_dev,),
        in_specs=[
            pl.BlockSpec((width, meridian_number), lambda s: (0, 0)),
            pl.BlockSpec((1, width), lambda s: (0, 0)),
        ]
        + table_specs,
        out_specs=slab,
        out_shape=exchange_shape,
        scratch_shapes=table_scratch,
        name="forward_dft",
    )(rows, live, coarse, fine)
    gathered = lax.all_to_all(modes, ("lat", "mem"), split_axis=0, concat_axis=0, tiled=True)

    own_orders = lax.dynamic_slice_in_dim(
        order_of_place, lax.axis_index(("lat", "mem")) * slot_dev, slot_dev
    )
    degree = jnp.arange(degrees, dtype=jnp.int32)
    valid = ((degree[None, :] >= own_orders[:, None]) & (degree[None, :] <= LMAX)).astype(
        jnp.float32
    )
    weight = field_importance[None, :, None] * valid[:, None, :]
    back = pl.pallas_call(
        functools.partial(score_kernel, bands, members, kinds, height),
        grid=(slot_dev,),
        in_specs=[
            slab,
            pl.BlockSpec((1, places, degrees), lambda s: (s, 0, 0)),
            pl.BlockSpec((1, 2, kinds, degrees), lambda s: (s, 0, 0, 0)),
            pl.BlockSpec((1, kinds, degrees), lambda s: (s, 0, 0)),
        ],
        out_specs=slab,
        out_shape=exchange_shape,
        scratch_shapes=[
            pltpu.VMEM((2 * kinds * members, places), jnp.bfloat16),
            pltpu.VMEM((degrees // LANES, 2 * kinds * members, LANES), jnp.float32),
        ],
        name="score_gradient",
    )(gathered, weighted_polynomial, truth_spectrum, weight)
    returned = lax.all_to_all(back, ("lat", "mem"), split_axis=0, concat_axis=0, tiled=True)

    field = pl.pallas_call(
        inverse_kernel,
        grid=(slot_dev,),
        in_specs=[pl.BlockSpec(memory_space=pltpu.SMEM), slab] + table_specs,
        out_specs=pl.BlockSpec((kinds, height, meridian_number), lambda s: (0, 0, 0)),
        out_shape=jax.ShapeDtypeStruct((kinds, height, meridian_number), jnp.bfloat16),
        scratch_shapes=table_scratch + [pltpu.VMEM((width, meridian_number), jnp.float32)],
        name="inverse_dft",
    )(own_rows[None], returned, coarse, fine)
    return field[None]


def solution(mesh):
    return jax.shard_map(
        local,
        mesh=mesh,
        in_specs=(
            P("mem", None, "lat", None),
            P(("lat", "mem"), None, None),
            P(("lat", "mem"), None, None, None),
            P(),
            P(),
            P(),
        ),
        out_specs=P("mem", None, "lat", None),
        check_vma=False,
    )
```

```python
import functools
import math

import jax
import jax.numpy as jnp
from jax import lax
from jax.experimental import pallas as pl
from jax.experimental.pallas import tpu as pltpu
from jax.sharding import PartitionSpec as P

LMAX = 720
EPS = 0.01
LANES = 128


BITS = 7


def angle_tables(orders, meridian_number):
    coarse_total = pl.cdiv(meridian_number, LANES)
    rows = 8 * pl.cdiv(BITS + coarse_total, 8)
    row = jnp.arange(rows, dtype=jnp.int32)[:, None]
    is_bit = row < BITS
    steps = jnp.where(is_bit, 1 << jnp.minimum(row, BITS), LANES * (row - BITS))
    product = steps * orders[None, :] % meridian_number
    angle = 2.0 * math.pi / meridian_number * product.astype(jnp.float32)
    used = (orders <= LMAX).astype(jnp.float32)[None, :] / math.sqrt(meridian_number)
    scale = jnp.where(is_bit, 1.0, used)
    return jnp.cos(angle) * scale, jnp.sin(angle) * scale


def turn(cos_a, sin_a, cos_b, sin_b):
    return cos_a * cos_b - sin_a * sin_b, sin_a * cos_b + cos_a * sin_b


def fill_tables(step_cos_ref, step_sin_ref, cos_ref, sin_ref):
    step_cos, step_sin = step_cos_ref[...].T, step_sin_ref[...].T
    slots, meridian_number = cos_ref.shape[1:]
    lane = lax.broadcasted_iota(jnp.int32, (slots, LANES), 1)
    fine_cos = jnp.ones((slots, LANES), jnp.float32)
    fine_sin = jnp.zeros((slots, LANES), jnp.float32)
    for bit in range(BITS):
        column = slice(bit, bit + 1)
        chosen = (lane & (1 << bit)) > 0
        bit_cos = jnp.where(chosen, step_cos[:, column], 1.0)
        bit_sin = jnp.where(chosen, step_sin[:, column], 0.0)
        fine_cos, fine_sin = turn(fine_cos, fine_sin, bit_cos, bit_sin)
    for j in range(pl.cdiv(meridian_number, LANES)):
        wide = min(LANES, meridian_number - j * LANES)
        column = slice(BITS + j, BITS + j + 1)
        cosine, sine = turn(fine_cos, fine_sin, step_cos[:, column], step_sin[:, column])
        at = slice(j * LANES, j * LANES + wide)
        cos_ref[0, :, at] = cosine[:, :wide].astype(jnp.bfloat16)
        sin_ref[0, :, at] = (-sine)[:, :wide].astype(jnp.bfloat16)


def forward_kernel(zone_ref, rows_ref, step_cos_ref, step_sin_ref, out_ref, cos_ref, sin_ref):
    fill_tables(step_cos_ref, step_sin_ref, cos_ref, sin_ref)
    kinds, height, meridian_number = rows_ref.shape
    width = kinds * height
    rows = rows_ref[...].reshape(width, meridian_number)
    own_rows = zone_ref[lax.axis_index("lat")]
    place = lax.broadcasted_iota(jnp.int32, (1, width), 1)
    for kind in range(kinds - 1, 0, -1):
        place = jnp.where(place >= kind * height, place - kind * height, place)
    live = (place < own_rows).astype(jnp.float32)
    for part, table in enumerate((cos_ref, sin_ref)):
        modes = lax.dot_general(
            table[0], rows, (((1,), (1,)), ((), ())), preferred_element_type=jnp.float32
        )
        out_ref[:, part * width : (part + 1) * width] = (modes * live).astype(jnp.bfloat16)


def inverse_kernel(zone_ref, back_ref, cos_ref, sin_ref, out_ref, total_ref):
    slot = pl.program_id(0)
    kinds, height, meridian_number = out_ref.shape
    width = kinds * height
    own_rows = zone_ref[lax.axis_index("lat")]
    term = jnp.zeros((width, meridian_number), jnp.float32)
    for part, table in enumerate((cos_ref, sin_ref)):
        term = term + lax.dot_general(
            back_ref[:, part * width : (part + 1) * width],
            table[0],
            (((0,), (0,)), ((), ())),
            preferred_element_type=jnp.float32,
        )

    @pl.when(slot == 0)
    def _():
        total_ref[...] = term

    @pl.when(slot > 0)
    def _():
        total_ref[...] += term

    @pl.when(slot == pl.num_programs(0) - 1)
    def _():
        place = lax.broadcasted_iota(jnp.int32, (height, meridian_number), 0)
        live = (place < own_rows).astype(jnp.float32)
        for kind in range(kinds):
            rows = total_ref[kind * height : (kind + 1) * height, :]
            out_ref[kind] = (rows * live).astype(jnp.bfloat16)


def exchange(slabs):
    devices, length = slabs.shape
    pieces = slabs.reshape(devices, 2, length // 2)
    pieces = lax.all_to_all(pieces, ("lat", "mem"), split_axis=0, concat_axis=0, tiled=True)
    return pieces.reshape(devices, length)


def kernel_grad(first, second):
    scale = lax.rsqrt(first * first + second * second + EPS)
    return first * scale, second * scale


def score_kernel(
    bands, members, kinds, height,
    spec_ref, poly_ref, truth_ref, weight_ref, out_ref, modes_ref, coeff_ref,
):
    width = kinds * height
    half = kinds * members
    tiles = coeff_ref.shape[0]

    for band in range(bands):
        source = slice(band * members, (band + 1) * members)
        for part in range(2):
            for kind in range(kinds):
                row = (part * kinds + kind) * members
                at = part * width + kind * height
                modes_ref[row : row + members, band * height : (band + 1) * height] = spec_ref[
                    source, at : at + height
                ]

    poly = poly_ref[0]
    coeffs = jnp.dot(modes_ref[...], poly, preferred_element_type=jnp.float32)
    for tile in range(tiles):
        coeff_ref[tile] = coeffs[:, tile * LANES : (tile + 1) * LANES]

    def per_tile(tile, carry):
        real = [coeff_ref[tile, pl.ds(m, kinds, stride=members), :] for m in range(members)]
        imag = [coeff_ref[tile, pl.ds(half + m, kinds, stride=members), :] for m in range(members)]
        pair_real = [jnp.zeros_like(real[0]) for _ in range(members)]
        pair_imag = [jnp.zeros_like(real[0]) for _ in range(members)]
        lanes = pl.ds(pl.multiple_of(tile * LANES, LANES), LANES)
        truth_real, truth_imag = truth_ref[0, 0, :, lanes], truth_ref[0, 1, :, lanes]
        weight = weight_ref[0, :, lanes]
        for m in range(members):
            for j in range(m + 1, members):
                first, second = kernel_grad(real[m] - real[j], imag[m] - imag[j])
                pair_real[m] = pair_real[m] + first
                pair_imag[m] = pair_imag[m] + second
                pair_real[j] = pair_real[j] - first
                pair_imag[j] = pair_imag[j] - second
            first, second = kernel_grad(real[m] - truth_real, imag[m] - truth_imag)
            coeff_ref[tile, pl.ds(m, kinds, stride=members), :] = weight * (
                first - pair_real[m] * (1.0 / members)
            )
            coeff_ref[tile, pl.ds(half + m, kinds, stride=members), :] = weight * (
                second - pair_imag[m] * (1.0 / members)
            )
        return carry

    lax.fori_loop(0, tiles, per_tile, 0)

    back = jnp.zeros(modes_ref.shape, jnp.float32)
    for tile in range(tiles):
        back = back + lax.dot_general(
            coeff_ref[tile].astype(jnp.bfloat16),
            poly[:, tile * LANES : (tile + 1) * LANES],
            (((1,), (1,)), ((), ())),
            preferred_element_type=jnp.float32,
        )
    modes_ref[...] = back.astype(jnp.bfloat16)

    for band in range(bands):
        target = slice(band * members, (band + 1) * members)
        for part in range(2):
            for kind in range(kinds):
                row = (part * kinds + kind) * members
                at = part * width + kind * height
                out_ref[target, at : at + height] = modes_ref[
                    row : row + members, band * height : (band + 1) * height
                ]


def local(
    predicted_fields,
    weighted_polynomial,
    truth_spectrum,
    field_importance,
    parallels_in_zone,
    order_of_place,
):
    _, kinds, height, meridian_number = predicted_fields.shape
    slot_dev, places, degrees = weighted_polynomial.shape
    slots = order_of_place.shape[0]
    devices = slots // slot_dev
    bands, members = lax.axis_size("lat"), lax.axis_size("mem")
    width = kinds * height
    orders = order_of_place.reshape(devices, slot_dev).T.reshape(slots)
    step_cos, step_sin = angle_tables(orders, meridian_number)
    step_spec = pl.BlockSpec((step_cos.shape[0], devices), lambda s: (0, s))
    table_spec = pl.BlockSpec((1, devices, meridian_number), lambda s: (s, 0, 0))
    table_shape = jax.ShapeDtypeStruct((slot_dev, devices, meridian_number), jnp.bfloat16)
    scalars = pl.BlockSpec(memory_space=pltpu.SMEM)
    exchange_shape = jax.ShapeDtypeStruct((devices, slot_dev * 2 * width), jnp.bfloat16)
    slab = pl.BlockSpec((devices, 2 * width), lambda s: (0, s))

    whole = pl.BlockSpec((kinds, height, meridian_number), lambda s: (0, 0, 0))
    modes, table_cos, table_sin = pl.pallas_call(
        forward_kernel,
        grid=(slot_dev,),
        in_specs=[scalars, whole, step_spec, step_spec],
        out_specs=[slab, table_spec, table_spec],
        out_shape=[exchange_shape, table_shape, table_shape],
        name="forward_dft",
    )(parallels_in_zone, predicted_fields[0], step_cos, step_sin)
    gathered = exchange(modes)

    own_orders = lax.dynamic_slice_in_dim(
        order_of_place, lax.axis_index(("lat", "mem")) * slot_dev, slot_dev
    )
    degree = jnp.arange(degrees, dtype=jnp.int32)
    valid = ((degree[None, :] >= own_orders[:, None]) & (degree[None, :] <= LMAX)).astype(
        jnp.float32
    )
    weight = field_importance[None, :, None] * valid[:, None, :]
    back = pl.pallas_call(
        functools.partial(score_kernel, bands, members, kinds, height),
        grid=(slot_dev,),
        in_specs=[
            slab,
            pl.BlockSpec((1, places, degrees), lambda s: (s, 0, 0)),
            pl.BlockSpec((1, 2, kinds, degrees), lambda s: (s, 0, 0, 0)),
            pl.BlockSpec((1, kinds, degrees), lambda s: (s, 0, 0)),
        ],
        out_specs=slab,
        out_shape=exchange_shape,
        scratch_shapes=[
            pltpu.VMEM((2 * kinds * members, places), jnp.bfloat16),
            pltpu.VMEM((degrees // LANES, 2 * kinds * members, LANES), jnp.float32),
        ],
        name="score_gradient",
    )(gathered, weighted_polynomial, truth_spectrum, weight)
    returned = exchange(back)

    field = pl.pallas_call(
        inverse_kernel,
        grid=(slot_dev,),
        in_specs=[scalars, slab, table_spec, table_spec],
        out_specs=whole,
        out_shape=jax.ShapeDtypeStruct((kinds, height, meridian_number), jnp.bfloat16),
        scratch_shapes=[pltpu.VMEM((width, meridian_number), jnp.float32)],
        name="inverse_dft",
    )(parallels_in_zone, returned, table_cos, table_sin)
    return field[None]


def solution(mesh):
    return jax.shard_map(
        local,
        mesh=mesh,
        in_specs=(
            P("mem", None, "lat", None),
            P(("lat", "mem"), None, None),
            P(("lat", "mem"), None, None, None),
            P(),
            P(),
            P(),
        ),
        out_specs=P("mem", None, "lat", None),
        check_vma=False,
    )
```

```python
import functools
import math

import jax
import jax.numpy as jnp
from jax import lax
from jax.experimental import pallas as pl
from jax.experimental.pallas import tpu as pltpu
from jax.sharding import PartitionSpec as P

LMAX = 720
EPS = 0.01
LANES = 128


BITS = 7


def angle_tables(orders, meridian_number):
    coarse_total = pl.cdiv(meridian_number, LANES)
    rows = 8 * pl.cdiv(BITS + coarse_total, 8)
    row = jnp.arange(rows, dtype=jnp.int32)[:, None]
    is_bit = row < BITS
    steps = jnp.where(is_bit, 1 << jnp.minimum(row, BITS), LANES * (row - BITS))
    product = steps * orders[None, :] % meridian_number
    angle = 2.0 * math.pi / meridian_number * product.astype(jnp.float32)
    used = (orders <= LMAX).astype(jnp.float32)[None, :] / math.sqrt(meridian_number)
    scale = jnp.where(is_bit, 1.0, used)
    return jnp.cos(angle) * scale, jnp.sin(angle) * scale


def turn(cos_a, sin_a, cos_b, sin_b):
    return cos_a * cos_b - sin_a * sin_b, sin_a * cos_b + cos_a * sin_b


def fill_tables(step_cos_ref, step_sin_ref, cos_ref, sin_ref):
    step_cos, step_sin = step_cos_ref[...].T, step_sin_ref[...].T
    slots, meridian_number = cos_ref.shape[1:]
    lane = lax.broadcasted_iota(jnp.int32, (slots, LANES), 1)
    fine_cos = jnp.ones((slots, LANES), jnp.float32)
    fine_sin = jnp.zeros((slots, LANES), jnp.float32)
    for bit in range(BITS):
        column = slice(bit, bit + 1)
        chosen = (lane & (1 << bit)) > 0
        bit_cos = jnp.where(chosen, step_cos[:, column], 1.0)
        bit_sin = jnp.where(chosen, step_sin[:, column], 0.0)
        fine_cos, fine_sin = turn(fine_cos, fine_sin, bit_cos, bit_sin)
    for j in range(pl.cdiv(meridian_number, LANES)):
        wide = min(LANES, meridian_number - j * LANES)
        column = slice(BITS + j, BITS + j + 1)
        cosine, sine = turn(fine_cos, fine_sin, step_cos[:, column], step_sin[:, column])
        at = slice(j * LANES, j * LANES + wide)
        cos_ref[0, :, at] = cosine[:, :wide].astype(jnp.bfloat16)
        sin_ref[0, :, at] = (-sine)[:, :wide].astype(jnp.bfloat16)


def fill_tables_down(step_cos_ref, step_sin_ref, cos_ref, sin_ref):
    meridian_number, slots = cos_ref.shape
    row = lax.broadcasted_iota(jnp.int32, (LANES, slots), 0)
    fine_cos = jnp.ones((LANES, slots), jnp.float32)
    fine_sin = jnp.zeros((LANES, slots), jnp.float32)
    for bit in range(BITS):
        at = slice(bit, bit + 1)
        chosen = (row & (1 << bit)) > 0
        bit_cos = jnp.where(chosen, step_cos_ref[at, :], 1.0)
        bit_sin = jnp.where(chosen, step_sin_ref[at, :], 0.0)
        fine_cos, fine_sin = turn(fine_cos, fine_sin, bit_cos, bit_sin)
    for j in range(pl.cdiv(meridian_number, LANES)):
        high = min(LANES, meridian_number - j * LANES)
        at = slice(BITS + j, BITS + j + 1)
        cosine, sine = turn(
            fine_cos[:high], fine_sin[:high], step_cos_ref[at, :], step_sin_ref[at, :]
        )
        cos_ref[j * LANES : j * LANES + high, :] = cosine.astype(jnp.bfloat16)
        sin_ref[j * LANES : j * LANES + high, :] = (-sine).astype(jnp.bfloat16)


def forward_kernel(zone_ref, rows_ref, step_cos_ref, step_sin_ref, out_ref, cos_ref, sin_ref):
    fill_tables_down(step_cos_ref, step_sin_ref, cos_ref, sin_ref)
    kinds, height, meridian_number = rows_ref.shape
    width = kinds * height
    rows = rows_ref[...].reshape(width, meridian_number)
    own_rows = zone_ref[lax.axis_index("lat")]
    place = lax.broadcasted_iota(jnp.int32, (1, width), 1)
    for kind in range(kinds - 1, 0, -1):
        place = jnp.where(place >= kind * height, place - kind * height, place)
    live = (place < own_rows).astype(jnp.float32)
    for part, table in enumerate((cos_ref, sin_ref)):
        modes = jnp.dot(rows, table[...], preferred_element_type=jnp.float32).T
        out_ref[:, part * width : (part + 1) * width] = (modes * live).astype(jnp.bfloat16)


def inverse_kernel(zone_ref, back_ref, cos_ref, sin_ref, out_ref, total_ref):
    slot = pl.program_id(0)
    kinds, height, meridian_number = out_ref.shape
    width = kinds * height
    own_rows = zone_ref[lax.axis_index("lat")]
    term = jnp.zeros((width, meridian_number), jnp.float32)
    for part, table in enumerate((cos_ref, sin_ref)):
        term = term + lax.dot_general(
            back_ref[:, part * width : (part + 1) * width],
            table[0],
            (((0,), (0,)), ((), ())),
            preferred_element_type=jnp.float32,
        )

    @pl.when(slot == 0)
    def _():
        total_ref[...] = term

    @pl.when(slot > 0)
    def _():
        total_ref[...] += term

    @pl.when(slot == pl.num_programs(0) - 1)
    def _():
        place = lax.broadcasted_iota(jnp.int32, (height, meridian_number), 0)
        live = (place < own_rows).astype(jnp.float32)
        for kind in range(kinds):
            rows = total_ref[kind * height : (kind + 1) * height, :]
            out_ref[kind] = (rows * live).astype(jnp.bfloat16)


def exchange(slabs):
    devices, length = slabs.shape
    halves = slabs.reshape(devices // 8, 8, 2, length // 2).transpose(0, 2, 1, 3)
    halves = lax.optimization_barrier(halves)
    pieces = halves.transpose(0, 2, 1, 3).reshape(devices, 2, length // 2)
    pieces = lax.all_to_all(pieces, ("lat", "mem"), split_axis=0, concat_axis=0, tiled=True)
    return pieces.reshape(devices, length)


def kernel_grad(first, second):
    scale = lax.rsqrt(first * first + second * second + EPS)
    return first * scale, second * scale


def score_kernel(
    bands, members, kinds, height,
    spec_ref, poly_ref, truth_ref, weight_ref, out_ref, modes_ref, coeff_ref,
):
    width = kinds * height
    half = kinds * members
    tiles = coeff_ref.shape[0]

    for band in range(bands):
        source = slice(band * members, (band + 1) * members)
        for part in range(2):
            for kind in range(kinds):
                row = (part * kinds + kind) * members
                at = part * width + kind * height
                modes_ref[row : row + members, band * height : (band + 1) * height] = spec_ref[
                    source, at : at + height
                ]

    poly = poly_ref[0]
    coeffs = jnp.dot(modes_ref[...], poly, preferred_element_type=jnp.float32)
    for tile in range(tiles):
        coeff_ref[tile] = coeffs[:, tile * LANES : (tile + 1) * LANES]

    def per_tile(tile, carry):
        real = [coeff_ref[tile, pl.ds(m, kinds, stride=members), :] for m in range(members)]
        imag = [coeff_ref[tile, pl.ds(half + m, kinds, stride=members), :] for m in range(members)]
        pair_real = [jnp.zeros_like(real[0]) for _ in range(members)]
        pair_imag = [jnp.zeros_like(real[0]) for _ in range(members)]
        lanes = pl.ds(pl.multiple_of(tile * LANES, LANES), LANES)
        truth_real, truth_imag = truth_ref[0, 0, :, lanes], truth_ref[0, 1, :, lanes]
        weight = weight_ref[0, :, lanes]
        for m in range(members):
            for j in range(m + 1, members):
                first, second = kernel_grad(real[m] - real[j], imag[m] - imag[j])
                pair_real[m] = pair_real[m] + first
                pair_imag[m] = pair_imag[m] + second
                pair_real[j] = pair_real[j] - first
                pair_imag[j] = pair_imag[j] - second
            first, second = kernel_grad(real[m] - truth_real, imag[m] - truth_imag)
            coeff_ref[tile, pl.ds(m, kinds, stride=members), :] = weight * (
                first - pair_real[m] * (1.0 / members)
            )
            coeff_ref[tile, pl.ds(half + m, kinds, stride=members), :] = weight * (
                second - pair_imag[m] * (1.0 / members)
            )
        return carry

    lax.fori_loop(0, tiles, per_tile, 0)

    back = jnp.zeros(modes_ref.shape, jnp.float32)
    for tile in range(tiles):
        back = back + lax.dot_general(
            coeff_ref[tile].astype(jnp.bfloat16),
            poly[:, tile * LANES : (tile + 1) * LANES],
            (((1,), (1,)), ((), ())),
            preferred_element_type=jnp.float32,
        )
    modes_ref[...] = back.astype(jnp.bfloat16)

    for band in range(bands):
        target = slice(band * members, (band + 1) * members)
        for part in range(2):
            for kind in range(kinds):
                row = (part * kinds + kind) * members
                at = part * width + kind * height
                out_ref[target, at : at + height] = modes_ref[
                    row : row + members, band * height : (band + 1) * height
                ]


def local(
    predicted_fields,
    weighted_polynomial,
    truth_spectrum,
    field_importance,
    parallels_in_zone,
    order_of_place,
):
    _, kinds, height, meridian_number = predicted_fields.shape
    slot_dev, places, degrees = weighted_polynomial.shape
    slots = order_of_place.shape[0]
    devices = slots // slot_dev
    bands, members = lax.axis_size("lat"), lax.axis_size("mem")
    width = kinds * height
    orders = order_of_place.reshape(devices, slot_dev).T.reshape(slots)
    step_cos, step_sin = angle_tables(orders, meridian_number)
    step_spec = pl.BlockSpec((step_cos.shape[0], devices), lambda s: (0, s))
    table_spec = pl.BlockSpec((1, devices, meridian_number), lambda s: (s, 0, 0))
    table_shape = jax.ShapeDtypeStruct((slot_dev, devices, meridian_number), jnp.bfloat16)
    scalars = pl.BlockSpec(memory_space=pltpu.SMEM)
    exchange_shape = jax.ShapeDtypeStruct((devices, slot_dev * 2 * width), jnp.bfloat16)
    slab = pl.BlockSpec((devices, 2 * width), lambda s: (0, s))

    whole = pl.BlockSpec((kinds, height, meridian_number), lambda s: (0, 0, 0))
    modes = pl.pallas_call(
        forward_kernel,
        grid=(slot_dev,),
        in_specs=[scalars, whole, step_spec, step_spec],
        out_specs=slab,
        out_shape=exchange_shape,
        scratch_shapes=[pltpu.VMEM((meridian_number, devices), jnp.bfloat16)] * 2,
        name="forward_dft",
    )(parallels_in_zone, predicted_fields[0], step_cos, step_sin)
    modes, step_cos, step_sin = lax.optimization_barrier((modes, step_cos, step_sin))
    table_cos, table_sin = pl.pallas_call(
        fill_tables,
        grid=(slot_dev,),
        in_specs=[step_spec, step_spec],
        out_specs=[table_spec, table_spec],
        out_shape=[table_shape, table_shape],
        cost_estimate=pl.CostEstimate(
            flops=8 * slots * meridian_number,
            bytes_accessed=4 * slots * meridian_number,
            transcendentals=0,
        ),
        name="inverse_tables",
    )(step_cos, step_sin)
    gathered = exchange(modes)

    own_orders = lax.dynamic_slice_in_dim(
        order_of_place, lax.axis_index(("lat", "mem")) * slot_dev, slot_dev
    )
    degree = jnp.arange(degrees, dtype=jnp.int32)
    valid = ((degree[None, :] >= own_orders[:, None]) & (degree[None, :] <= LMAX)).astype(
        jnp.float32
    )
    weight = field_importance[None, :, None] * valid[:, None, :]
    back = pl.pallas_call(
        functools.partial(score_kernel, bands, members, kinds, height),
        grid=(slot_dev,),
        in_specs=[
            slab,
            pl.BlockSpec((1, places, degrees), lambda s: (s, 0, 0)),
            pl.BlockSpec((1, 2, kinds, degrees), lambda s: (s, 0, 0, 0)),
            pl.BlockSpec((1, kinds, degrees), lambda s: (s, 0, 0)),
        ],
        out_specs=slab,
        out_shape=exchange_shape,
        scratch_shapes=[
            pltpu.VMEM((2 * kinds * members, places), jnp.bfloat16),
            pltpu.VMEM((degrees // LANES, 2 * kinds * members, LANES), jnp.float32),
        ],
        name="score_gradient",
    )(gathered, weighted_polynomial, truth_spectrum, weight)
    returned = exchange(back)

    field = pl.pallas_call(
        inverse_kernel,
        grid=(slot_dev,),
        in_specs=[scalars, slab, table_spec, table_spec],
        out_specs=whole,
        out_shape=jax.ShapeDtypeStruct((kinds, height, meridian_number), jnp.bfloat16),
        scratch_shapes=[pltpu.VMEM((width, meridian_number), jnp.float32)],
        name="inverse_dft",
    )(parallels_in_zone, returned, table_cos, table_sin)
    return field[None]


def solution(mesh):
    return jax.shard_map(
        local,
        mesh=mesh,
        in_specs=(
            P("mem", None, "lat", None),
            P(("lat", "mem"), None, None),
            P(("lat", "mem"), None, None, None),
            P(),
            P(),
            P(),
        ),
        out_specs=P("mem", None, "lat", None),
        check_vma=False,
    )
```

```python
import functools
import math

import jax
import jax.numpy as jnp
from jax import lax
from jax.experimental import pallas as pl
from jax.experimental.pallas import tpu as pltpu
from jax.sharding import PartitionSpec as P

LMAX = 720
EPS = 0.01
LANES = 128
VMEM_LIMIT = 24 * 2**20


BITS = 7


def angle_tables(orders, meridian_number):
    coarse_total = pl.cdiv(meridian_number, LANES)
    rows = 8 * pl.cdiv(BITS + coarse_total, 8)
    row = jnp.arange(rows, dtype=jnp.int32)[:, None]
    is_bit = row < BITS
    steps = jnp.where(is_bit, 1 << jnp.minimum(row, BITS), LANES * (row - BITS))
    product = steps * orders[None, :] % meridian_number
    angle = 2.0 * math.pi / meridian_number * product.astype(jnp.float32)
    used = (orders <= LMAX).astype(jnp.float32)[None, :] / math.sqrt(meridian_number)
    scale = jnp.where(is_bit, 1.0, used)
    return jnp.cos(angle) * scale, jnp.sin(angle) * scale


def turn(cos_a, sin_a, cos_b, sin_b):
    return cos_a * cos_b - sin_a * sin_b, sin_a * cos_b + cos_a * sin_b


def fill_tables(step_cos_ref, step_sin_ref, table_ref):
    step_cos, step_sin = step_cos_ref[...].T, step_sin_ref[...].T
    slots, meridian_number = table_ref.shape[2:]
    lane = lax.broadcasted_iota(jnp.int32, (slots, LANES), 1)
    fine_cos = jnp.ones((slots, LANES), jnp.float32)
    fine_sin = jnp.zeros((slots, LANES), jnp.float32)
    for bit in range(BITS):
        column = slice(bit, bit + 1)
        chosen = (lane & (1 << bit)) > 0
        bit_cos = jnp.where(chosen, step_cos[:, column], 1.0)
        bit_sin = jnp.where(chosen, step_sin[:, column], 0.0)
        fine_cos, fine_sin = turn(fine_cos, fine_sin, bit_cos, bit_sin)
    for j in range(pl.cdiv(meridian_number, LANES)):
        wide = min(LANES, meridian_number - j * LANES)
        column = slice(BITS + j, BITS + j + 1)
        cosine, sine = turn(fine_cos, fine_sin, step_cos[:, column], step_sin[:, column])
        at = slice(j * LANES, j * LANES + wide)
        table_ref[0, 0, :, at] = cosine[:, :wide].astype(jnp.bfloat16)
        table_ref[0, 1, :, at] = (-sine)[:, :wide].astype(jnp.bfloat16)


def fill_tables_down(step_cos_ref, step_sin_ref, cos_ref, sin_ref):
    meridian_number, slots = cos_ref.shape
    row = lax.broadcasted_iota(jnp.int32, (LANES, slots), 0)
    fine_cos = jnp.ones((LANES, slots), jnp.float32)
    fine_sin = jnp.zeros((LANES, slots), jnp.float32)
    for bit in range(BITS):
        at = slice(bit, bit + 1)
        chosen = (row & (1 << bit)) > 0
        bit_cos = jnp.where(chosen, step_cos_ref[at, :], 1.0)
        bit_sin = jnp.where(chosen, step_sin_ref[at, :], 0.0)
        fine_cos, fine_sin = turn(fine_cos, fine_sin, bit_cos, bit_sin)
    for j in range(pl.cdiv(meridian_number, LANES)):
        high = min(LANES, meridian_number - j * LANES)
        at = slice(BITS + j, BITS + j + 1)
        cosine, sine = turn(
            fine_cos[:high], fine_sin[:high], step_cos_ref[at, :], step_sin_ref[at, :]
        )
        cos_ref[j * LANES : j * LANES + high, :] = cosine.astype(jnp.bfloat16)
        sin_ref[j * LANES : j * LANES + high, :] = (-sine).astype(jnp.bfloat16)


def forward_kernel(zone_ref, rows_ref, step_cos_ref, step_sin_ref, out_ref, cos_ref, sin_ref):
    fill_tables_down(step_cos_ref, step_sin_ref, cos_ref, sin_ref)
    kinds, height, meridian_number = rows_ref.shape
    width = kinds * height
    rows = rows_ref[...].reshape(width, meridian_number)
    own_rows = zone_ref[lax.axis_index("lat")]
    place = lax.broadcasted_iota(jnp.int32, (1, width), 1)
    for kind in range(kinds - 1, 0, -1):
        place = jnp.where(place >= kind * height, place - kind * height, place)
    live = (place < own_rows).astype(jnp.float32)
    for part, table in enumerate((cos_ref, sin_ref)):
        modes = jnp.dot(rows, table[...], preferred_element_type=jnp.float32).T
        out_ref[:, part * width : (part + 1) * width] = (modes * live).astype(jnp.bfloat16)


def inverse_kernel(zone_ref, back_ref, table_ref, out_ref, flat_ref):
    kinds, height, wide = out_ref.shape
    width = kinds * height
    devices, length = back_ref.shape
    own_rows = zone_ref[lax.axis_index("lat")]

    @pl.when(pl.program_id(0) == 0)
    def _():
        for piece in range(length // width):
            block = back_ref[:, piece * width : (piece + 1) * width].astype(jnp.float32)
            flat_ref[:, piece * devices : (piece + 1) * devices] = block.T.astype(jnp.bfloat16)

    field = jnp.dot(flat_ref[...], table_ref[...], preferred_element_type=jnp.float32)
    live = lax.broadcasted_iota(jnp.int32, (height, wide), 0) < own_rows
    for kind in range(kinds):
        rows = field[kind * height : (kind + 1) * height, :]
        out_ref[kind] = (rows * live.astype(jnp.float32)).astype(jnp.bfloat16)


def exchange(slabs):
    devices, length = slabs.shape
    halves = slabs.reshape(devices // 8, 8, 2, length // 2).transpose(0, 2, 1, 3)
    halves = lax.optimization_barrier(halves)
    pieces = halves.transpose(0, 2, 1, 3).reshape(devices, 2, length // 2)
    pieces = lax.all_to_all(pieces, ("lat", "mem"), split_axis=0, concat_axis=0, tiled=True)
    return pieces.reshape(devices, length)


def kernel_grad(first, second):
    scale = lax.rsqrt(first * first + second * second + EPS)
    return first * scale, second * scale


def score_kernel(
    bands, members, kinds, height,
    spec_ref, poly_ref, truth_ref, weight_ref, out_ref, modes_ref, coeff_ref,
):
    width = kinds * height
    half = kinds * members
    tiles = coeff_ref.shape[0]

    for band in range(bands):
        source = slice(band * members, (band + 1) * members)
        for part in range(2):
            for kind in range(kinds):
                row = (part * kinds + kind) * members
                at = part * width + kind * height
                modes_ref[row : row + members, band * height : (band + 1) * height] = spec_ref[
                    source, at : at + height
                ]

    poly = poly_ref[0]
    modes = modes_ref[...]

    def legendre(tile):
        columns = poly[:, tile * LANES : (tile + 2) * LANES]
        coeffs = jnp.dot(modes, columns, preferred_element_type=jnp.float32)
        coeff_ref[tile] = coeffs[:, :LANES]
        coeff_ref[tile + 1] = coeffs[:, LANES:]

    def per_tile(tile, carry):
        real = [coeff_ref[tile, pl.ds(m, kinds, stride=members), :] for m in range(members)]
        imag = [coeff_ref[tile, pl.ds(half + m, kinds, stride=members), :] for m in range(members)]
        pair_real = [jnp.zeros_like(real[0]) for _ in range(members)]
        pair_imag = [jnp.zeros_like(real[0]) for _ in range(members)]
        lanes = slice(tile * LANES, (tile + 1) * LANES)
        truth_real, truth_imag = truth_ref[0, 0, :, lanes], truth_ref[0, 1, :, lanes]
        weight = weight_ref[0, :, lanes]
        for m in range(members):
            for j in range(m + 1, members):
                first, second = kernel_grad(real[m] - real[j], imag[m] - imag[j])
                pair_real[m] = pair_real[m] + first
                pair_imag[m] = pair_imag[m] + second
                pair_real[j] = pair_real[j] - first
                pair_imag[j] = pair_imag[j] - second
            first, second = kernel_grad(real[m] - truth_real, imag[m] - truth_imag)
            coeff_ref[tile, pl.ds(m, kinds, stride=members), :] = weight * (
                first - pair_real[m] * (1.0 / members)
            )
            coeff_ref[tile, pl.ds(half + m, kinds, stride=members), :] = weight * (
                second - pair_imag[m] * (1.0 / members)
            )
        return carry

    legendre(0)
    for tile in range(0, tiles, 2):
        if tile + 2 < tiles:
            legendre(tile + 2)
        per_tile(tile, 0)
        per_tile(tile + 1, 0)

    grads = jnp.concatenate([coeff_ref[tile].astype(jnp.bfloat16) for tile in range(tiles)], axis=1)
    back = lax.dot_general(
        grads, poly, (((1,), (1,)), ((), ())), preferred_element_type=jnp.float32
    )
    modes_ref[...] = back.astype(jnp.bfloat16)

    for band in range(bands):
        target = slice(band * members, (band + 1) * members)
        for part in range(2):
            for kind in range(kinds):
                row = (part * kinds + kind) * members
                at = part * width + kind * height
                out_ref[target, at : at + height] = modes_ref[
                    row : row + members, band * height : (band + 1) * height
                ]


def local(
    predicted_fields,
    weighted_polynomial,
    truth_spectrum,
    field_importance,
    parallels_in_zone,
    order_of_place,
):
    _, kinds, height, meridian_number = predicted_fields.shape
    slot_dev, places, degrees = weighted_polynomial.shape
    slots = order_of_place.shape[0]
    devices = slots // slot_dev
    bands, members = lax.axis_size("lat"), lax.axis_size("mem")
    width = kinds * height
    orders = order_of_place.reshape(devices, slot_dev).T.reshape(slots)
    step_cos, step_sin = angle_tables(orders, meridian_number)
    step_spec = pl.BlockSpec((step_cos.shape[0], devices), lambda s: (0, s))
    scalars = pl.BlockSpec(memory_space=pltpu.SMEM)
    exchange_shape = jax.ShapeDtypeStruct((devices, slot_dev * 2 * width), jnp.bfloat16)
    slab = pl.BlockSpec((devices, 2 * width), lambda s: (0, s))

    whole = pl.BlockSpec((kinds, height, meridian_number), lambda s: (0, 0, 0))
    modes = pl.pallas_call(
        forward_kernel,
        grid=(slot_dev,),
        in_specs=[scalars, whole, step_spec, step_spec],
        out_specs=slab,
        out_shape=exchange_shape,
        scratch_shapes=[pltpu.VMEM((meridian_number, devices), jnp.bfloat16)] * 2,
        compiler_params=pltpu.CompilerParams(vmem_limit_bytes=VMEM_LIMIT),
        name="forward_dft",
    )(parallels_in_zone, predicted_fields[0], step_cos, step_sin)
    modes, step_cos, step_sin = lax.optimization_barrier((modes, step_cos, step_sin))
    table = pl.pallas_call(
        fill_tables,
        grid=(slot_dev,),
        in_specs=[step_spec, step_spec],
        out_specs=pl.BlockSpec((1, 2, devices, meridian_number), lambda s: (s, 0, 0, 0)),
        out_shape=jax.ShapeDtypeStruct((slot_dev, 2, devices, meridian_number), jnp.bfloat16),
        cost_estimate=pl.CostEstimate(
            flops=8 * slots * meridian_number,
            bytes_accessed=4 * slots * meridian_number,
            transcendentals=0,
        ),
        name="inverse_tables",
    )(step_cos, step_sin)
    gathered = exchange(modes)

    own_orders = lax.dynamic_slice_in_dim(
        order_of_place, lax.axis_index(("lat", "mem")) * slot_dev, slot_dev
    )
    degree = jnp.arange(degrees, dtype=jnp.int32)
    valid = ((degree[None, :] >= own_orders[:, None]) & (degree[None, :] <= LMAX)).astype(
        jnp.float32
    )
    weight = field_importance[None, :, None] * valid[:, None, :]
    back = pl.pallas_call(
        functools.partial(score_kernel, bands, members, kinds, height),
        grid=(slot_dev,),
        in_specs=[
            slab,
            pl.BlockSpec((1, places, degrees), lambda s: (s, 0, 0)),
            pl.BlockSpec((1, 2, kinds, degrees), lambda s: (s, 0, 0, 0)),
            pl.BlockSpec((1, kinds, degrees), lambda s: (s, 0, 0)),
        ],
        out_specs=slab,
        out_shape=exchange_shape,
        scratch_shapes=[
            pltpu.VMEM((2 * kinds * members, places), jnp.bfloat16),
            pltpu.VMEM((degrees // LANES, 2 * kinds * members, LANES), jnp.float32),
        ],
        compiler_params=pltpu.CompilerParams(vmem_limit_bytes=VMEM_LIMIT),
        name="score_gradient",
    )(gathered, weighted_polynomial, truth_spectrum, weight)
    returned = exchange(back)

    wide = 3 * LANES
    field = pl.pallas_call(
        inverse_kernel,
        grid=(pl.cdiv(meridian_number, wide),),
        in_specs=[
            scalars,
            pl.BlockSpec((devices, slot_dev * 2 * width), lambda n: (0, 0)),
            pl.BlockSpec((2 * slots, wide), lambda n: (0, n)),
        ],
        out_specs=pl.BlockSpec((kinds, height, wide), lambda n: (0, 0, n)),
        out_shape=jax.ShapeDtypeStruct((kinds, height, meridian_number), jnp.bfloat16),
        scratch_shapes=[pltpu.VMEM((width, 2 * slots), jnp.bfloat16)],
        compiler_params=pltpu.CompilerParams(vmem_limit_bytes=59 * 2**20),
        name="inverse_dft",
    )(parallels_in_zone, returned, table.reshape(2 * slots, meridian_number))
    return field[None]


def solution(mesh):
    return jax.shard_map(
        local,
        mesh=mesh,
        in_specs=(
            P("mem", None, "lat", None),
            P(("lat", "mem"), None, None),
            P(("lat", "mem"), None, None, None),
            P(),
            P(),
            P(),
        ),
        out_specs=P("mem", None, "lat", None),
        check_vma=False,
    )
```

```python
import functools
import math

import jax
import jax.numpy as jnp
from jax import lax
from jax.experimental import pallas as pl
from jax.experimental.pallas import tpu as pltpu
from jax.sharding import PartitionSpec as P

LMAX = 720
EPS = 0.01
LANES = 128
VMEM_LIMIT = 24 * 2**20


BITS = 7


def angle_tables(orders, meridian_number):
    coarse_total = pl.cdiv(meridian_number, LANES)
    rows = 8 * pl.cdiv(BITS + coarse_total, 8)
    row = jnp.arange(rows, dtype=jnp.int32)[:, None]
    is_bit = row < BITS
    steps = jnp.where(is_bit, 1 << jnp.minimum(row, BITS), LANES * (row - BITS))
    product = steps * orders[None, :] % meridian_number
    angle = 2.0 * math.pi / meridian_number * product.astype(jnp.float32)
    used = (orders <= LMAX).astype(jnp.float32)[None, :] / math.sqrt(meridian_number)
    scale = jnp.where(is_bit, 1.0, used)
    return jnp.cos(angle) * scale, jnp.sin(angle) * scale


def turn(cos_a, sin_a, cos_b, sin_b):
    return cos_a * cos_b - sin_a * sin_b, sin_a * cos_b + cos_a * sin_b


def fill_tables(step_cos_ref, step_sin_ref, table_ref):
    step_cos, step_sin = step_cos_ref[...].T, step_sin_ref[...].T
    slots, meridian_number = table_ref.shape[2:]
    lane = lax.broadcasted_iota(jnp.int32, (slots, LANES), 1)
    fine_cos = jnp.ones((slots, LANES), jnp.float32)
    fine_sin = jnp.zeros((slots, LANES), jnp.float32)
    for bit in range(BITS):
        column = slice(bit, bit + 1)
        chosen = (lane & (1 << bit)) > 0
        bit_cos = jnp.where(chosen, step_cos[:, column], 1.0)
        bit_sin = jnp.where(chosen, step_sin[:, column], 0.0)
        fine_cos, fine_sin = turn(fine_cos, fine_sin, bit_cos, bit_sin)
    for j in range(pl.cdiv(meridian_number, LANES)):
        wide = min(LANES, meridian_number - j * LANES)
        column = slice(BITS + j, BITS + j + 1)
        cosine, sine = turn(fine_cos, fine_sin, step_cos[:, column], step_sin[:, column])
        at = slice(j * LANES, j * LANES + wide)
        table_ref[0, 0, :, at] = cosine[:, :wide].astype(jnp.bfloat16)
        table_ref[0, 1, :, at] = (-sine)[:, :wide].astype(jnp.bfloat16)


def fill_tables_down(step_cos_ref, step_sin_ref, cos_ref, sin_ref):
    meridian_number, slots = cos_ref.shape
    row = lax.broadcasted_iota(jnp.int32, (LANES, slots), 0)
    fine_cos = jnp.ones((LANES, slots), jnp.float32)
    fine_sin = jnp.zeros((LANES, slots), jnp.float32)
    for bit in range(BITS):
        at = slice(bit, bit + 1)
        chosen = (row & (1 << bit)) > 0
        bit_cos = jnp.where(chosen, step_cos_ref[at, :], 1.0)
        bit_sin = jnp.where(chosen, step_sin_ref[at, :], 0.0)
        fine_cos, fine_sin = turn(fine_cos, fine_sin, bit_cos, bit_sin)
    for j in range(pl.cdiv(meridian_number, LANES)):
        high = min(LANES, meridian_number - j * LANES)
        at = slice(BITS + j, BITS + j + 1)
        cosine, sine = turn(
            fine_cos[:high], fine_sin[:high], step_cos_ref[at, :], step_sin_ref[at, :]
        )
        cos_ref[j * LANES : j * LANES + high, :] = cosine.astype(jnp.bfloat16)
        sin_ref[j * LANES : j * LANES + high, :] = (-sine).astype(jnp.bfloat16)


def forward_kernel(zone_ref, rows_ref, step_cos_ref, step_sin_ref, out_ref, cos_ref, sin_ref):
    fill_tables_down(step_cos_ref, step_sin_ref, cos_ref, sin_ref)
    kinds, height, meridian_number = rows_ref.shape
    width = kinds * height
    rows = rows_ref[...].reshape(width, meridian_number)
    own_rows = zone_ref[lax.axis_index("lat")]
    place = lax.broadcasted_iota(jnp.int32, (1, width), 1)
    for kind in range(kinds - 1, 0, -1):
        place = jnp.where(place >= kind * height, place - kind * height, place)
    live = (place < own_rows).astype(jnp.float32)
    for part, table in enumerate((cos_ref, sin_ref)):
        modes = jnp.dot(rows, table[...], preferred_element_type=jnp.float32).T
        out_ref[:, part * width : (part + 1) * width] = (modes * live).astype(jnp.bfloat16)


def inverse_kernel(zone_ref, back_ref, table_ref, out_ref, flat_ref):
    kinds, height, wide = out_ref.shape
    width = kinds * height
    devices, length = back_ref.shape
    own_rows = zone_ref[lax.axis_index("lat")]

    @pl.when(pl.program_id(0) == 0)
    def _():
        for piece in range(length // width):
            block = back_ref[:, piece * width : (piece + 1) * width].astype(jnp.float32)
            flat_ref[:, piece * devices : (piece + 1) * devices] = block.T.astype(jnp.bfloat16)

    field = jnp.dot(flat_ref[...], table_ref[...], preferred_element_type=jnp.float32)
    live = lax.broadcasted_iota(jnp.int32, (height, wide), 0) < own_rows
    for kind in range(kinds):
        rows = field[kind * height : (kind + 1) * height, :]
        out_ref[kind] = (rows * live.astype(jnp.float32)).astype(jnp.bfloat16)


def exchange(slabs):
    devices, length = slabs.shape
    halves = slabs.reshape(devices // 8, 8, 2, length // 2).transpose(0, 2, 1, 3)
    halves = lax.optimization_barrier(halves)
    pieces = halves.transpose(0, 2, 1, 3).reshape(devices, 2, length // 2)
    pieces = lax.all_to_all(pieces, ("lat", "mem"), split_axis=0, concat_axis=0, tiled=True)
    return pieces.reshape(devices, length)


def kernel_grad(first, second):
    scale = lax.rsqrt(first * first + second * second + EPS)
    return first * scale, second * scale


def score_kernel(
    bands, members, kinds, height,
    spec_ref, poly_ref, truth_ref, weight_ref, out_ref, modes_ref, coeff_ref,
):
    width = kinds * height
    half = kinds * members
    tiles = coeff_ref.shape[0]

    for band in range(bands):
        source = slice(band * members, (band + 1) * members)
        for part in range(2):
            for kind in range(kinds):
                row = (part * kinds + kind) * members
                at = part * width + kind * height
                modes_ref[row : row + members, band * height : (band + 1) * height] = spec_ref[
                    source, at : at + height
                ]

    poly = poly_ref[0]
    modes = modes_ref[...]

    def legendre(tile):
        columns = poly[:, tile * LANES : (tile + 2) * LANES]
        coeffs = jnp.dot(modes, columns, preferred_element_type=jnp.float32)
        coeff_ref[tile] = coeffs[:, :LANES]
        coeff_ref[tile + 1] = coeffs[:, LANES:]

    def per_tile(tile, carry):
        real = [coeff_ref[tile, pl.ds(m, kinds, stride=members), :] for m in range(members)]
        imag = [coeff_ref[tile, pl.ds(half + m, kinds, stride=members), :] for m in range(members)]
        pair_real = [jnp.zeros_like(real[0]) for _ in range(members)]
        pair_imag = [jnp.zeros_like(real[0]) for _ in range(members)]
        lanes = slice(tile * LANES, (tile + 1) * LANES)
        truth_real, truth_imag = truth_ref[0, 0, :, lanes], truth_ref[0, 1, :, lanes]
        weight = weight_ref[0, :, lanes]
        for m in range(members):
            for j in range(m + 1, members):
                first, second = kernel_grad(real[m] - real[j], imag[m] - imag[j])
                pair_real[m] = pair_real[m] + first
                pair_imag[m] = pair_imag[m] + second
                pair_real[j] = pair_real[j] - first
                pair_imag[j] = pair_imag[j] - second
            first, second = kernel_grad(real[m] - truth_real, imag[m] - truth_imag)
            coeff_ref[tile, pl.ds(m, kinds, stride=members), :] = weight * (
                first - pair_real[m] * (1.0 / members)
            )
            coeff_ref[tile, pl.ds(half + m, kinds, stride=members), :] = weight * (
                second - pair_imag[m] * (1.0 / members)
            )
        return carry

    legendre(0)
    for tile in range(0, tiles, 2):
        if tile + 2 < tiles:
            legendre(tile + 2)
        per_tile(tile, 0)
        per_tile(tile + 1, 0)

    grads = jnp.concatenate([coeff_ref[tile].astype(jnp.bfloat16) for tile in range(tiles)], axis=1)
    back = lax.dot_general(
        grads, poly, (((1,), (1,)), ((), ())), preferred_element_type=jnp.float32
    )
    modes_ref[...] = back.astype(jnp.bfloat16)

    for band in range(bands):
        target = slice(band * members, (band + 1) * members)
        for part in range(2):
            for kind in range(kinds):
                row = (part * kinds + kind) * members
                at = part * width + kind * height
                out_ref[target, at : at + height] = modes_ref[
                    row : row + members, band * height : (band + 1) * height
                ]


def local(
    predicted_fields,
    weighted_polynomial,
    truth_spectrum,
    field_importance,
    parallels_in_zone,
    order_of_place,
):
    _, kinds, height, meridian_number = predicted_fields.shape
    slot_dev, places, degrees = weighted_polynomial.shape
    slots = order_of_place.shape[0]
    devices = slots // slot_dev
    bands, members = lax.axis_size("lat"), lax.axis_size("mem")
    width = kinds * height
    orders = order_of_place.reshape(devices, slot_dev).T.reshape(slots)
    step_cos, step_sin = angle_tables(orders, meridian_number)
    step_spec = pl.BlockSpec((step_cos.shape[0], devices), lambda s: (0, s))
    scalars = pl.BlockSpec(memory_space=pltpu.SMEM)
    exchange_shape = jax.ShapeDtypeStruct((devices, slot_dev * 2 * width), jnp.bfloat16)
    slab = pl.BlockSpec((devices, 2 * width), lambda s: (0, s))

    whole = pl.BlockSpec((kinds, height, meridian_number), lambda s: (0, 0, 0))
    modes = pl.pallas_call(
        forward_kernel,
        grid=(slot_dev,),
        in_specs=[scalars, whole, step_spec, step_spec],
        out_specs=slab,
        out_shape=exchange_shape,
        scratch_shapes=[pltpu.VMEM((meridian_number, devices), jnp.bfloat16)] * 2,
        compiler_params=pltpu.CompilerParams(vmem_limit_bytes=VMEM_LIMIT),
        name="forward_dft",
    )(parallels_in_zone, predicted_fields[0], step_cos, step_sin)
    modes, step_cos, step_sin = lax.optimization_barrier((modes, step_cos, step_sin))
    table = pl.pallas_call(
        fill_tables,
        grid=(slot_dev,),
        in_specs=[step_spec, step_spec],
        out_specs=pl.BlockSpec((1, 2, devices, meridian_number), lambda s: (s, 0, 0, 0)),
        out_shape=jax.ShapeDtypeStruct((slot_dev, 2, devices, meridian_number), jnp.bfloat16),
        cost_estimate=pl.CostEstimate(
            flops=8 * slots * meridian_number,
            bytes_accessed=4 * slots * meridian_number,
            transcendentals=0,
        ),
        name="inverse_tables",
    )(step_cos, step_sin)
    gathered = exchange(modes)

    own_orders = lax.dynamic_slice_in_dim(
        order_of_place, lax.axis_index(("lat", "mem")) * slot_dev, slot_dev
    )
    degree = jnp.arange(degrees, dtype=jnp.int32)
    valid = ((degree[None, :] >= own_orders[:, None]) & (degree[None, :] <= LMAX)).astype(
        jnp.float32
    )
    weight = field_importance[None, :, None] * valid[:, None, :]
    back = pl.pallas_call(
        functools.partial(score_kernel, bands, members, kinds, height),
        grid=(slot_dev,),
        in_specs=[
            slab,
            pl.BlockSpec((1, places, degrees), lambda s: (s, 0, 0)),
            pl.BlockSpec((1, 2, kinds, degrees), lambda s: (s, 0, 0, 0)),
            pl.BlockSpec((1, kinds, degrees), lambda s: (s, 0, 0)),
        ],
        out_specs=slab,
        out_shape=exchange_shape,
        scratch_shapes=[
            pltpu.VMEM((2 * kinds * members, places), jnp.bfloat16),
            pltpu.VMEM((degrees // LANES, 2 * kinds * members, LANES), jnp.float32),
        ],
        compiler_params=pltpu.CompilerParams(vmem_limit_bytes=VMEM_LIMIT),
        name="score_gradient",
    )(gathered, weighted_polynomial, truth_spectrum, weight)
    returned = exchange(back)

    wide = 4 * LANES
    field = pl.pallas_call(
        inverse_kernel,
        grid=(pl.cdiv(meridian_number, wide),),
        in_specs=[
            scalars,
            pl.BlockSpec((devices, slot_dev * 2 * width), lambda n: (0, 0)),
            pl.BlockSpec((2 * slots, wide), lambda n: (0, n)),
        ],
        out_specs=pl.BlockSpec((kinds, height, wide), lambda n: (0, 0, n)),
        out_shape=jax.ShapeDtypeStruct((kinds, height, meridian_number), jnp.bfloat16),
        scratch_shapes=[pltpu.VMEM((width, 2 * slots), jnp.bfloat16)],
        compiler_params=pltpu.CompilerParams(vmem_limit_bytes=59 * 2**20),
        name="inverse_dft",
    )(parallels_in_zone, returned, table.reshape(2 * slots, meridian_number))
    return field[None]


def solution(mesh):
    return jax.shard_map(
        local,
        mesh=mesh,
        in_specs=(
            P("mem", None, "lat", None),
            P(("lat", "mem"), None, None),
            P(("lat", "mem"), None, None, None),
            P(),
            P(),
            P(),
        ),
        out_specs=P("mem", None, "lat", None),
        check_vma=False,
    )
```
